128 devices in a mesh: row: 8 (over x, core), col: 16 (over z, y).
Axes of the slice: x: 4, y: 4, z: 4, core: 2. Of those that a mesh axis runs over, the one named last changes fastest.
Arguments:
- matrix: float32 [16384, 16384], P('row', 'col'), may hold values from -40 to 40
Outputs:
- r_rows: float32 [512, 16384], P(None, 'col')
- scaled_basis: float32 [16384, 512], P('row')
- trailing: float32 [16384, 16384], P('row', 'col')
The draws below stay inside these ranges and needn't reach their ends.
All inputs are finite; a program needn't handle non-finite values.
Results may differ from the reference program's by a relative error of at most 0.00013.
Values sent between devices are 32-bit elements; how exact they have to be, the bound alone decides.
No kernel may reach another device: no remote copies, remote signals or barrier semaphores. Data moves between devices by JAX's collectives and lax.ppermute only.
A program may use at most 128 MiB of HBM per device.

```python
import math
import jax
import jax.numpy as jnp
from jax import lax

N = 16384
B = 256
PANELS = 2
M = 16384
N_COL = 16


def draw_matrix(key, part):
    key_entries = jax.random.fold_in(key, 11)
    key_rows = jax.random.fold_in(key, 12)
    key_cols = jax.random.fold_in(key, 13)
    key_shared = jax.random.fold_in(key, 14)
    groups = (N + B - 1) // B
    share = 0.35
    remainder = math.sqrt(1.0 - share * share)
    row_scale = jnp.exp(jax.random.uniform(key_rows, (M, 1), jnp.float32) * math.log(10.0))
    col_scale = jnp.exp(jax.random.uniform(key_cols, (1, N), jnp.float32) * math.log(10.0))
    shared = jax.random.normal(key_shared, (M, groups), jnp.float32)
    noise = jax.random.normal(key_entries, (M, N), jnp.float32)
    spread = jnp.repeat(shared, B, axis=1)[:, :N]
    entries = jnp.clip(share * spread + remainder * noise, -4.0, 4.0)
    return 0.1 * entries * row_scale * col_scale


def setup_inputs(seed: int = 0) -> dict:
    keys = jax.random.split(jax.random.key(seed), 2)
    matrix = draw_matrix(jax.random.fold_in(keys[1], 71), 0)
    return {"matrix": matrix}


def product(left, right):
    return jnp.dot(left, right, precision=lax.Precision.HIGHEST)

def reference(matrix):
    current = matrix
    block_cols = N // N_COL
    r_blocks = []
    basis_blocks = []
    for panel_index in range(PANELS):
        panel_cols = current[:, panel_index * block_cols:panel_index * block_cols + B]
        gram_matrix = product(panel_cols.T, panel_cols)
        lower_factor = jnp.linalg.cholesky(gram_matrix)
        orthonormal = jax.scipy.linalg.solve_triangular(lower_factor, panel_cols.T, lower=True).T
        coupling = product(orthonormal.T, current)
        current = current - product(orthonormal, coupling)
        r_blocks.append(coupling)
        basis_blocks.append(orthonormal * math.sqrt(M))
    return (jnp.concatenate(r_blocks, axis=0), jnp.concatenate(basis_blocks, axis=1), current)
```

```python
import functools
import math

import jax
import jax.numpy as jnp
from jax import lax
from jax.experimental import pallas as pl
from jax.experimental.pallas import tpu as pltpu
from jax.sharding import PartitionSpec as P

B = 256
PANELS = 2
SIDE = 4
BLOCK = 128
SUB = 8


HIGHEST = lax.Precision.HIGHEST
HIGH = lax.Precision.HIGH
CORE_SWAP = [(i, i ^ 1) for i in range(2 * SIDE)]
PAIRS_A = [(2 * x + c, 2 * (x ^ 1) + c) for x in range(SIDE) for c in range(2)]
PAIRS_B = [(2 * x + c, 2 * (3 - x) + c) for x in range(SIDE) for c in range(2)]


def ring(axis, step):
    if axis == "y":
        return [(z * SIDE + y, z * SIDE + (y + step) % SIDE) for z in range(SIDE) for y in range(SIDE)]
    return [(z * SIDE + y, (z + step) % SIDE * SIDE + y) for z in range(SIDE) for y in range(SIDE)]


def take_half(x, upper):
    half = x.shape[0] // 2
    return lax.dynamic_slice_in_dim(x, upper * half, half, 0)


def put_halves(mine, other, upper):
    flag = upper == 1
    return jnp.concatenate([jnp.where(flag, other, mine), jnp.where(flag, mine, other)], axis=0)


def row_sum(x):
    place = lax.axis_index("row")
    core = place % 2
    chip = place // 2
    bit_a = ((chip == 1) | (chip == 2)).astype(jnp.int32)
    bit_b = (chip >= 2).astype(jnp.int32)
    kept = take_half(x, core) + lax.ppermute(take_half(x, 1 - core), "row", CORE_SWAP)
    half = kept.shape[0] // 2
    parts = []
    plans = ((kept[:half], PAIRS_A, bit_a, PAIRS_B, bit_b), (kept[half:], PAIRS_B, bit_b, PAIRS_A, bit_a))
    for part, pairs_1, bit_1, pairs_2, bit_2 in plans:
        part = take_half(part, bit_1) + lax.ppermute(take_half(part, 1 - bit_1), "row", pairs_1)
        part = take_half(part, bit_2) + lax.ppermute(take_half(part, 1 - bit_2), "row", pairs_2)
        part = put_halves(part, lax.ppermute(part, "row", pairs_2), bit_2)
        part = put_halves(part, lax.ppermute(part, "row", pairs_1), bit_1)
        parts.append(part)
    kept = jnp.concatenate(parts, axis=0)
    return put_halves(kept, lax.ppermute(kept, "row", CORE_SWAP), core)


def scatter(own):
    col = lax.axis_index("col")
    count = SIDE * SIDE
    rows = own.shape[0] // count
    mine = lax.dynamic_slice_in_dim(own, col * rows, rows, 0)
    first = jnp.where(col == 0, mine, 0.0)
    second = jnp.where(col == 1, mine, 0.0)
    for i in range(1, count):
        piece = lax.dynamic_slice_in_dim(own, (i + col) % count * rows, rows, 0)
        got = lax.ppermute(piece, "col", [(0, i), (1, (i + 1) % count)])
        first = jnp.where(col == i, got, first)
        second = jnp.where(col == (i + 1) % count, got, second)
    return jnp.concatenate([first, second], axis=1)


def ring_gather(x, axis):
    half = x.shape[0] // 2
    before = lax.ppermute(x, "col", ring(axis, 1))
    after = lax.ppermute(x, "col", ring(axis, -1))
    far_1 = lax.ppermute(before[:half], "col", ring(axis, 1))
    far_2 = lax.ppermute(after[half:], "col", ring(axis, -1))
    return [x, after, jnp.concatenate([far_1, far_2], axis=0), before]


def place_gather(x, axis, spot):
    pieces = ring_gather(x, axis)
    out = jnp.zeros((SIDE,) + x.shape, x.dtype)
    for step, piece in enumerate(pieces):
        out = lax.dynamic_update_index_in_dim(out, piece, (spot + step) % SIDE, 0)
    return out


def gather_panels(piece):
    col = lax.axis_index("col")
    y = col % SIDE
    z = col // SIDE
    rows, width = piece.shape
    half = rows // 2
    part_a = place_gather(piece[:half], "y", y)
    part_b = place_gather(piece[half:], "z", z)
    part_a = place_gather(part_a.reshape(SIDE * half, width), "z", z)
    part_b = place_gather(part_b.reshape(SIDE * half, width), "y", y)
    part_a = part_a.reshape(SIDE, SIDE, 1, half, width)
    part_b = part_b.reshape(SIDE, SIDE, 1, half, width).transpose(1, 0, 2, 3, 4)
    return jnp.concatenate([part_a, part_b], axis=2).reshape(SIDE * SIDE * rows, width)


def inverse_factor_kernel(gram_ref, out_ref, work):
    size = gram_ref.shape[0]
    work[...] = gram_ref[...]
    lane = lax.broadcasted_iota(jnp.int32, (SUB, BLOCK), 1)
    sub = lax.broadcasted_iota(jnp.int32, (SUB, BLOCK), 0)
    tiles_n = BLOCK // SUB

    def block_step(k, carry):
        start = pl.multiple_of(k * BLOCK, BLOCK)
        tiles = [work[pl.ds(start + t * SUB, SUB), pl.ds(start, BLOCK)] for t in range(tiles_n)]
        for j in range(BLOCK):
            a, s = j // SUB, j % SUB
            at_j = lane == j
            row = jnp.broadcast_to(tiles[a][s:s + 1, :], (SUB, BLOCK))
            pivot = jnp.broadcast_to(row[:, j:j + 1], (SUB, BLOCK))
            scaled = jnp.where(at_j, 1.0, row) * pl.reciprocal(pivot, approx=False)
            for t in range(a, tiles_n):
                if t == a and s == SUB - 1:
                    continue
                factor = jnp.broadcast_to(tiles[t][:, j:j + 1], (SUB, BLOCK))
                new = jnp.where(at_j, 0.0, tiles[t]) - factor * scaled
                tiles[t] = jnp.where(sub > s, new, tiles[t]) if t == a else new
        rows = []
        for t in range(tiles_n):
            diag = lane == sub + t * SUB
            pivot = jnp.sum(jnp.where(diag, tiles[t], 0.0), axis=1, keepdims=True)
            root = lax.rsqrt(pivot)
            root = root * (1.5 - 0.5 * pivot * root * root)
            lower = jnp.where(lane < sub + t * SUB, tiles[t], 0.0)
            rows.append(jnp.where(diag, 1.0, lower) * root)
        block_inverse = jnp.concatenate(rows, axis=0)
        strip = jnp.dot(block_inverse, work[pl.ds(start, BLOCK), :], precision=HIGHEST, preferred_element_type=jnp.float32)
        work[pl.ds(start, BLOCK), :] = strip
        upper = work[pl.ds(start, BLOCK), :]
        work[pl.ds(start, BLOCK), pl.ds(start, BLOCK)] = block_inverse
        strip = work[pl.ds(start, BLOCK), :]
        row_id = lax.broadcasted_iota(jnp.int32, (size, size), 0)
        col_id = lax.broadcasted_iota(jnp.int32, (size, size), 1)
        below = row_id >= start + BLOCK
        change = lax.dot_general(upper, strip, (((0,), (0,)), ((), ())), precision=HIGHEST, preferred_element_type=jnp.float32)
        in_block = (col_id >= start) & (col_id < start + BLOCK)
        base = jnp.where(in_block, 0.0, work[...])
        work[...] = jnp.where(below, base - change, work[...])
        return carry

    lax.fori_loop(0, size // BLOCK, block_step, 0)
    row_id = lax.broadcasted_iota(jnp.int32, (size, size), 0)
    col_id = lax.broadcasted_iota(jnp.int32, (size, size), 1)
    out_ref[...] = jnp.where(row_id >= col_id, work[...], 0.0)


def inverse_factor(gram):
    size = gram.shape[0]
    return pl.pallas_call(
        inverse_factor_kernel,
        out_shape=jax.ShapeDtypeStruct((size, size), jnp.float32),
        in_specs=[pl.BlockSpec(memory_space=pltpu.VMEM)],
        out_specs=pl.BlockSpec(memory_space=pltpu.VMEM),
        scratch_shapes=[pltpu.VMEM((size, size), jnp.float32)],
        name="inverse_factor",
    )(gram)


def on_device(matrix):
    root_rows = math.sqrt(matrix.shape[0] * lax.axis_size("row"))
    panels = gather_panels(scatter(matrix[:, :B]))
    left, right = panels[:, :B], panels[:, B:]
    gram_wide = jnp.dot(left.T, panels, precision=HIGHEST)
    gram_last = jnp.dot(right.T, right, precision=HIGHEST)
    gram = row_sum(jnp.concatenate([gram_wide, gram_last], axis=1))
    across = gram[:, B:2 * B]
    full = jnp.concatenate(
        [gram[:, :2 * B], jnp.concatenate([across.T, gram[:, 2 * B:]], axis=1)], axis=0)
    coupling = row_sum(jnp.dot(panels.T, matrix, precision=HIGH))
    inverse = inverse_factor(full)
    basis = jnp.dot(panels, inverse.T * root_rows, precision=HIGH)
    r_rows = jnp.dot(inverse, coupling, precision=HIGH)
    trailing = matrix - jnp.dot(basis, r_rows * (1.0 / root_rows), precision=HIGH)
    return (r_rows, basis, trailing)


def solution(mesh):
    placed = (P("row", "col"),)
    return jax.shard_map(
        on_device,
        mesh=mesh,
        in_specs=placed,
        out_specs=(P(None, "col"), P("row", None), P("row", "col")),
        check_vma=False,
    )
```

```python
import functools
import math

import jax
import jax.numpy as jnp
from jax import lax
from jax.experimental import pallas as pl
from jax.experimental.pallas import tpu as pltpu
from jax.sharding import PartitionSpec as P

B = 256
PANELS = 2
SIDE = 4
BLOCK = 128
SUB = 8
STRIDE = 2


HIGHEST = lax.Precision.HIGHEST
HIGH = lax.Precision.HIGH
CORE_SWAP = [(i, i ^ 1) for i in range(2 * SIDE)]
PAIRS_A = [(2 * x + c, 2 * (x ^ 1) + c) for x in range(SIDE) for c in range(2)]
PAIRS_B = [(2 * x + c, 2 * (3 - x) + c) for x in range(SIDE) for c in range(2)]


def ring(axis, step):
    if axis == "y":
        return [(z * SIDE + y, z * SIDE + (y + step) % SIDE) for z in range(SIDE) for y in range(SIDE)]
    return [(z * SIDE + y, (z + step) % SIDE * SIDE + y) for z in range(SIDE) for y in range(SIDE)]


def half_of(x, upper):
    half = x.shape[0] // 2
    return lax.dynamic_slice_in_dim(x, upper * half, half, 0)


def put_halves(mine, other, upper):
    flag = upper == 1
    return jnp.concatenate([jnp.where(flag, other, mine), jnp.where(flag, mine, other)], axis=0)


def pair_sum(x):
    core = lax.axis_index("row") % 2
    return half_of(x, core) + lax.ppermute(half_of(x, 1 - core), "row", CORE_SWAP)


def tie(*values):
    return lax.optimization_barrier(values)


def swap_start(parts, swap_1, swap_2):
    return lax.ppermute(parts[0], "row", swap_1), lax.ppermute(parts[1], "row", swap_2)


def add_all(mine, theirs):
    return [a + b for a, b in zip(mine, theirs)]


def columns_of(x, upper):
    return lax.dynamic_slice_in_dim(x, upper * B, B, 1)


def pair_join(parts):
    core = lax.axis_index("row") % 2
    kept = jnp.concatenate(parts, axis=0)
    return put_halves(kept, lax.ppermute(kept, "row", CORE_SWAP), core)


def split(x):
    half = x.shape[0] // 2
    return x[:half], x[half:]


def scatter(own):
    col = lax.axis_index("col")
    count = SIDE * SIDE
    rows = own.shape[0] // count
    mine = lax.dynamic_slice_in_dim(own, col * rows, rows, 0)
    first = jnp.where(col == 0, mine, 0.0)
    second = jnp.where(col == 1, mine, 0.0)
    for i in range(1, count):
        piece = lax.dynamic_slice_in_dim(own, (i + col) % count * rows, rows, 0)
        got = lax.ppermute(piece, "col", [(0, i), (1, (i + 1) % count)])
        first = jnp.where(col == i, got, first)
        second = jnp.where(col == (i + 1) % count, got, second)
    return jnp.concatenate([first, second], axis=1)


def ring_gather(x, axis):
    half = x.shape[0] // 2
    before = lax.ppermute(x, "col", ring(axis, 1))
    after = lax.ppermute(x, "col", ring(axis, -1))
    far_1 = lax.ppermute(before[:half], "col", ring(axis, 1))
    far_2 = lax.ppermute(after[half:], "col", ring(axis, -1))
    return [x, after, jnp.concatenate([far_1, far_2], axis=0), before]


def place_gather(x, axis, spot):
    pieces = ring_gather(x, axis)
    out = jnp.zeros((SIDE,) + x.shape, x.dtype)
    for step, piece in enumerate(pieces):
        out = lax.dynamic_update_index_in_dim(out, piece, (spot + step) % SIDE, 0)
    return out


def gather_panels(piece):
    col = lax.axis_index("col")
    y = col % SIDE
    z = col // SIDE
    rows, width = piece.shape
    half = rows // 2
    part_a = place_gather(piece[:half], "y", y)
    part_b = place_gather(piece[half:], "z", z)
    part_a = place_gather(part_a.reshape(SIDE * half, width), "z", z)
    part_b = place_gather(part_b.reshape(SIDE * half, width), "y", y)
    part_a = part_a.reshape(SIDE, SIDE, 1, half, width)
    part_b = part_b.reshape(SIDE, SIDE, 1, half, width).transpose(1, 0, 2, 3, 4)
    return jnp.concatenate([part_a, part_b], axis=2).reshape(SIDE * SIDE * rows, width)


def inverse_factor_kernel(first_block, last, state_ref, out_ref, block):
    size = state_ref.shape[0]
    out_ref[...] = state_ref[...]
    lane = lax.broadcasted_iota(jnp.int32, (SUB, BLOCK), 1)
    sub = lax.broadcasted_iota(jnp.int32, (SUB, BLOCK), 0)
    tiles_n = BLOCK // SUB
    low = first_block * BLOCK
    span = size - low

    def panel_steps(begin, end):
        tiles = {t: block[t * SUB:(t + 1) * SUB, :] for t in range(begin, tiles_n)}
        for a in range(begin, end):
            first = a * SUB
            in_panel = (lane >= first) & (lane < first + SUB)
            panel = jnp.where(in_panel, 0.0, tiles[a])
            cols = [jnp.broadcast_to(tiles[a][:, first + s:first + s + 1], (SUB, BLOCK)) for s in range(SUB)]
            pivots = jnp.zeros((SUB, BLOCK), jnp.float32)
            scaled, ratios = [], {}
            for s in range(SUB):
                pivot = jnp.broadcast_to(cols[s][s:s + 1, :], (SUB, BLOCK))
                pivots = jnp.where(sub == s, pivot, pivots)
                inverse = pl.reciprocal(pivot, approx=False)
                row = jnp.broadcast_to(panel[s:s + 1, :], (SUB, BLOCK))
                scaled.append(jnp.where(lane == first + s, 1.0, row) * inverse)
                factor = jnp.where(sub > s, cols[s], 0.0)
                for u in range(s + 1, SUB):
                    ratios[s, u] = jnp.broadcast_to(cols[u][s:s + 1, :], (SUB, BLOCK)) * inverse
                    cols[u] = cols[u] - factor * ratios[s, u]
                panel = panel - factor * scaled[s]
            root = lax.rsqrt(pivots)
            root = root * (1.5 - 0.5 * pivots * root * root)
            lower = jnp.where(lane < sub + first, panel, 0.0)
            block[first:first + SUB, :] = jnp.where(lane == sub + first, 1.0, lower) * root
            for t in range(a + 1, tiles_n):
                cols = [jnp.broadcast_to(tiles[t][:, first + s:first + s + 1], (SUB, BLOCK)) for s in range(SUB)]
                tile = jnp.where(in_panel, 0.0, tiles[t])
                for s in range(SUB):
                    for u in range(s + 1, SUB):
                        cols[u] = cols[u] - cols[s] * ratios[s, u]
                    tile = tile - cols[s] * scaled[s]
                tiles[t] = tile
        for t in range(end, tiles_n):
            block[t * SUB:(t + 1) * SUB, :] = tiles[t]

    def block_step(k, carry):
        start = pl.multiple_of(k * BLOCK, BLOCK)
        block[...] = out_ref[pl.ds(start, BLOCK), pl.ds(start, BLOCK)]
        for begin in range(0, tiles_n, STRIDE):
            pl.when(k >= 0)(functools.partial(panel_steps, begin, begin + STRIDE))
        strip = jnp.dot(block[...], out_ref[pl.ds(start, BLOCK), :], precision=HIGHEST, preferred_element_type=jnp.float32)
        out_ref[pl.ds(start, BLOCK), :] = strip
        out_ref[pl.ds(start, BLOCK), pl.ds(start, BLOCK)] = block[...]
        full = out_ref[pl.ds(start, BLOCK), :]
        row_id = low + lax.broadcasted_iota(jnp.int32, (span, size), 0)
        col_id = lax.broadcasted_iota(jnp.int32, (span, size), 1)
        change = lax.dot_general(
            strip[:, low:], full, (((0,), (0,)), ((), ())), precision=HIGHEST, preferred_element_type=jnp.float32)
        in_block = (col_id >= start) & (col_id < start + BLOCK)
        now = out_ref[low:, :]
        out_ref[low:, :] = jnp.where(row_id >= start + BLOCK, jnp.where(in_block, 0.0, now) - change, now)
        return carry

    lax.fori_loop(first_block, last, block_step, 0)
    if last * BLOCK == size:
        row_id = lax.broadcasted_iota(jnp.int32, (size, size), 0)
        col_id = lax.broadcasted_iota(jnp.int32, (size, size), 1)
        out_ref[...] = jnp.where(row_id >= col_id, out_ref[...], 0.0)


def factor_part(state, first_block, last):
    size = state.shape[0]
    return pl.pallas_call(
        functools.partial(inverse_factor_kernel, first_block, last),
        out_shape=jax.ShapeDtypeStruct((size, size), jnp.float32),
        in_specs=[pl.BlockSpec(memory_space=pltpu.VMEM)],
        out_specs=pl.BlockSpec(memory_space=pltpu.VMEM),
        scratch_shapes=[pltpu.VMEM((BLOCK, BLOCK), jnp.float32)],
        cost_estimate=pl.CostEstimate(flops=6 * 10**9, transcendentals=0, bytes_accessed=2 * 10**6),
        name=f"inverse_factor_{first_block}",
    )(state)


def inverse_factor(gram):
    middle = gram.shape[0] // BLOCK // 2
    return factor_part(factor_part(gram, 0, middle), middle, 2 * middle)


def on_device(matrix):
    root_rows = math.sqrt(matrix.shape[0] * lax.axis_size("row"))
    panels = gather_panels(scatter(matrix[:, :B]))
    left, right = panels[:, :B], panels[:, B:]
    core = lax.axis_index("row") % 2
    gram_wide = jnp.dot(left.T, panels, precision=HIGHEST)
    gram_last = jnp.dot(right.T, right, precision=HIGHEST)
    gram = pair_sum(jnp.concatenate([gram_wide, gram_last], axis=1))
    moved = swap_start(split(gram), PAIRS_A, PAIRS_B)
    other = jnp.dot(columns_of(panels, 1 - core).T, matrix, precision=HIGH)
    gram, moved, other = tie(split(gram), moved, other)
    gram = add_all(gram, moved)
    moved = swap_start(gram, PAIRS_B, PAIRS_A)
    mine = jnp.dot(columns_of(panels, core).T, matrix, precision=HIGH)
    moved, mine = tie(moved, mine)
    gram = pair_join(add_all(gram, moved))
    across = gram[:, B:2 * B]
    full = jnp.concatenate(
        [gram[:, :2 * B], jnp.concatenate([across.T, gram[:, 2 * B:]], axis=1)], axis=0)
    mine, full = tie(mine + lax.ppermute(other, "row", CORE_SWAP), full)
    middle = full.shape[0] // BLOCK // 2
    parts = split(mine)
    moved = swap_start(parts, PAIRS_A, PAIRS_B)
    state = factor_part(full, 0, middle)
    moved, state = tie(moved, state)
    parts = add_all(parts, moved)
    moved = swap_start(parts, PAIRS_B, PAIRS_A)
    inverse = factor_part(state, middle, 2 * middle)
    moved, inverse = tie(moved, inverse)
    mine = jnp.concatenate(add_all(parts, moved), axis=0)
    other = lax.ppermute(mine, "row", CORE_SWAP)
    r_mine = jnp.dot(columns_of(inverse, core), mine, precision=HIGH)
    basis = jnp.dot(panels, inverse.T * root_rows, precision=HIGH)
    other, r_mine, basis = tie(other, r_mine, basis)
    r_rows = r_mine + jnp.dot(columns_of(inverse, 1 - core), other, precision=HIGH)
    trailing = matrix - jnp.dot(basis, r_rows * (1.0 / root_rows), precision=HIGH)
    return (r_rows, basis, trailing)


def solution(mesh):
    placed = (P("row", "col"),)
    return jax.shard_map(
        on_device,
        mesh=mesh,
        in_specs=placed,
        out_specs=(P(None, "col"), P("row", None), P("row", "col")),
        check_vma=False,
    )
```

```python
import functools
import math

import jax
import jax.numpy as jnp
from jax import lax
from jax.experimental import pallas as pl
from jax.experimental.pallas import tpu as pltpu
from jax.sharding import PartitionSpec as P

B = 256
PANELS = 2
SIDE = 4
BLOCK = 128
SUB = 8
STRIDE = 2


HIGHEST = lax.Precision.HIGHEST
HIGH = lax.Precision.HIGH
CORE_SWAP = [(i, i ^ 1) for i in range(2 * SIDE)]
PAIRS_A = [(2 * x + c, 2 * (x ^ 1) + c) for x in range(SIDE) for c in range(2)]
PAIRS_B = [(2 * x + c, 2 * (3 - x) + c) for x in range(SIDE) for c in range(2)]


def ring(axis, step):
    if axis == "y":
        return [(z * SIDE + y, z * SIDE + (y + step) % SIDE) for z in range(SIDE) for y in range(SIDE)]
    return [(z * SIDE + y, (z + step) % SIDE * SIDE + y) for z in range(SIDE) for y in range(SIDE)]


def half_of(x, upper):
    half = x.shape[0] // 2
    return lax.dynamic_slice_in_dim(x, upper * half, half, 0)


def tie(*values):
    return lax.optimization_barrier(values)


def swap_start(parts, swap_1, swap_2):
    return lax.ppermute(parts[0], "row", swap_1), lax.ppermute(parts[1], "row", swap_2)


def add_all(mine, theirs):
    return [a + b for a, b in zip(mine, theirs)]


def columns_of(x, upper):
    return lax.dynamic_slice_in_dim(x, upper * B, B, 1)


def split(x):
    half = x.shape[0] // 2
    return x[:half], x[half:]


def scatter(own):
    col = lax.axis_index("col")
    first_core = lax.axis_index("row") % 2 == 0
    count = SIDE * SIDE
    rows = own.shape[0] // count
    before = (col + count - 1) % count
    step_1 = jnp.where(first_core, before, col)
    step_2 = jnp.where(first_core, col, before)
    mine = lax.dynamic_slice_in_dim(own, col * rows, rows, 0)
    slot_1 = jnp.where(step_1 == 0, mine, 0.0)
    slot_2 = jnp.where(step_2 == 0, mine, 0.0)
    for i in range(1, count):
        piece = lax.dynamic_slice_in_dim(own, (i + col) % count * rows, rows, 0)
        got = lax.ppermute(piece, "col", [(0, i), (1, (i + 1) % count)])
        slot_1 = jnp.where(step_1 == i, got, slot_1)
        slot_2 = jnp.where(step_2 == i, got, slot_2)
    return jnp.concatenate([slot_1, slot_2], axis=1)


def ring_gather(x, axis):
    half = x.shape[0] // 2
    before = lax.ppermute(x, "col", ring(axis, 1))
    after = lax.ppermute(x, "col", ring(axis, -1))
    far_1 = lax.ppermute(before[:half], "col", ring(axis, 1))
    far_2 = lax.ppermute(after[half:], "col", ring(axis, -1))
    return [x, after, jnp.concatenate([far_1, far_2], axis=0), before]


def place_gather(x, axis, spot):
    pieces = ring_gather(x, axis)
    out = jnp.zeros((SIDE,) + x.shape, x.dtype)
    for step, piece in enumerate(pieces):
        out = lax.dynamic_update_index_in_dim(out, piece, (spot + step) % SIDE, 0)
    return out


def gather_panels(piece):
    col = lax.axis_index("col")
    y = col % SIDE
    z = col // SIDE
    rows, width = piece.shape
    half = rows // 2
    part_a = place_gather(piece[:half], "y", y)
    part_b = place_gather(piece[half:], "z", z)
    part_a = place_gather(part_a.reshape(SIDE * half, width), "z", z)
    part_b = place_gather(part_b.reshape(SIDE * half, width), "y", y)
    part_a = part_a.reshape(SIDE, SIDE, 1, half, width)
    part_b = part_b.reshape(SIDE, SIDE, 1, half, width).transpose(1, 0, 2, 3, 4)
    return jnp.concatenate([part_a, part_b], axis=2).reshape(SIDE * SIDE * rows, width)


def inverse_factor_kernel(first_block, last, state_ref, out_ref, block):
    size = state_ref.shape[0]
    out_ref[...] = state_ref[...]
    lane = lax.broadcasted_iota(jnp.int32, (SUB, BLOCK), 1)
    sub = lax.broadcasted_iota(jnp.int32, (SUB, BLOCK), 0)
    tiles_n = BLOCK // SUB
    low = first_block * BLOCK
    span = size - low

    def panel_steps(begin, end):
        tiles = {t: block[t * SUB:(t + 1) * SUB, :] for t in range(begin, tiles_n)}
        for a in range(begin, end):
            first = a * SUB
            in_panel = (lane >= first) & (lane < first + SUB)
            panel = jnp.where(in_panel, 0.0, tiles[a])
            cols = [jnp.broadcast_to(tiles[a][:, first + s:first + s + 1], (SUB, BLOCK)) for s in range(SUB)]
            pivots = jnp.zeros((SUB, BLOCK), jnp.float32)
            scaled, ratios = [], {}
            for s in range(SUB):
                pivot = jnp.broadcast_to(cols[s][s:s + 1, :], (SUB, BLOCK))
                pivots = jnp.where(sub == s, pivot, pivots)
                inverse = pl.reciprocal(pivot, approx=False)
                row = jnp.broadcast_to(panel[s:s + 1, :], (SUB, BLOCK))
                scaled.append(jnp.where(lane == first + s, 1.0, row) * inverse)
                factor = jnp.where(sub > s, cols[s], 0.0)
                for u in range(s + 1, SUB):
                    ratios[s, u] = jnp.broadcast_to(cols[u][s:s + 1, :], (SUB, BLOCK)) * inverse
                    cols[u] = cols[u] - factor * ratios[s, u]
                panel = panel - factor * scaled[s]
            root = lax.rsqrt(pivots)
            root = root * (1.5 - 0.5 * pivots * root * root)
            lower = jnp.where(lane < sub + first, panel, 0.0)
            block[first:first + SUB, :] = jnp.where(lane == sub + first, 1.0, lower) * root
            for t in range(a + 1, tiles_n):
                cols = [jnp.broadcast_to(tiles[t][:, first + s:first + s + 1], (SUB, BLOCK)) for s in range(SUB)]
                tile = jnp.where(in_panel, 0.0, tiles[t])
                for s in range(SUB):
                    for u in range(s + 1, SUB):
                        cols[u] = cols[u] - cols[s] * ratios[s, u]
                    tile = tile - cols[s] * scaled[s]
                tiles[t] = tile
        for t in range(end, tiles_n):
            block[t * SUB:(t + 1) * SUB, :] = tiles[t]

    def block_step(k, carry):
        start = pl.multiple_of(k * BLOCK, BLOCK)
        block[...] = out_ref[pl.ds(start, BLOCK), pl.ds(start, BLOCK)]
        for begin in range(0, tiles_n, STRIDE):
            pl.when(k >= 0)(functools.partial(panel_steps, begin, begin + STRIDE))
        strip = jnp.dot(block[...], out_ref[pl.ds(start, BLOCK), :], precision=HIGHEST, preferred_element_type=jnp.float32)
        out_ref[pl.ds(start, BLOCK), :] = strip
        out_ref[pl.ds(start, BLOCK), pl.ds(start, BLOCK)] = block[...]
        full = out_ref[pl.ds(start, BLOCK), :]
        row_id = low + lax.broadcasted_iota(jnp.int32, (span, size), 0)
        col_id = lax.broadcasted_iota(jnp.int32, (span, size), 1)
        change = lax.dot_general(
            strip[:, low:], full, (((0,), (0,)), ((), ())), precision=HIGHEST, preferred_element_type=jnp.float32)
        in_block = (col_id >= start) & (col_id < start + BLOCK)
        now = out_ref[low:, :]
        out_ref[low:, :] = jnp.where(row_id >= start + BLOCK, jnp.where(in_block, 0.0, now) - change, now)
        return carry

    lax.fori_loop(first_block, last, block_step, 0)
    if last * BLOCK == size:
        row_id = lax.broadcasted_iota(jnp.int32, (size, size), 0)
        col_id = lax.broadcasted_iota(jnp.int32, (size, size), 1)
        out_ref[...] = jnp.where(row_id >= col_id, out_ref[...], 0.0)


def factor_part(state, first_block, last):
    size = state.shape[0]
    return pl.pallas_call(
        functools.partial(inverse_factor_kernel, first_block, last),
        out_shape=jax.ShapeDtypeStruct((size, size), jnp.float32),
        in_specs=[pl.BlockSpec(memory_space=pltpu.VMEM)],
        out_specs=pl.BlockSpec(memory_space=pltpu.VMEM),
        scratch_shapes=[pltpu.VMEM((BLOCK, BLOCK), jnp.float32)],
        cost_estimate=pl.CostEstimate(flops=6 * 10**9, transcendentals=0, bytes_accessed=2 * 10**6),
        name=f"inverse_factor_{first_block}",
    )(state)


def inverse_factor(gram):
    middle = gram.shape[0] // BLOCK // 2
    return factor_part(factor_part(gram, 0, middle), middle, 2 * middle)


def on_device(matrix):
    root_rows = math.sqrt(matrix.shape[0] * lax.axis_size("row"))
    panels = gather_panels(scatter(matrix[:, :B]))
    core = lax.axis_index("row") % 2
    first_core = core == 0
    gram = jnp.dot(panels.T, panels, precision=HIGHEST)
    cross = jnp.where(first_core, gram[B:, :B], gram[:B, B:])
    kept = jnp.concatenate([gram[B:, B:], half_of(cross, core)], axis=0)
    sent = jnp.concatenate([gram[:B, :B], half_of(cross, 1 - core)], axis=0)
    gram = split(kept + lax.ppermute(sent, "row", CORE_SWAP))
    moved = swap_start(gram, PAIRS_A, PAIRS_B)
    coupling = jnp.dot(panels.T, matrix, precision=HIGH)
    moved, coupling = tie(moved, coupling)
    gram = add_all(gram, moved)
    other, mine = split(coupling)
    moved = swap_start(gram, PAIRS_B, PAIRS_A)
    mine = mine + lax.ppermute(other, "row", CORE_SWAP)
    moved, mine = tie(moved, mine)
    gram = jnp.concatenate(add_all(gram, moved), axis=0)
    theirs = lax.ppermute(gram, "row", CORE_SWAP)
    left, right = jnp.where(first_core, gram, theirs), jnp.where(first_core, theirs, gram)
    cross = jnp.concatenate([left[B:], right[B:]], axis=0)
    full = jnp.concatenate([
        jnp.concatenate([left[:B], cross], axis=1),
        jnp.concatenate([cross, right[:B]], axis=1)], axis=0)
    mine, full = tie(mine, full)
    middle = full.shape[0] // BLOCK // 2
    parts = split(mine)
    moved = swap_start(parts, PAIRS_A, PAIRS_B)
    state = factor_part(full, 0, middle)
    moved, state = tie(moved, state)
    parts = add_all(parts, moved)
    moved = swap_start(parts, PAIRS_B, PAIRS_A)
    inverse = factor_part(state, middle, 2 * middle)
    moved, inverse = tie(moved, inverse)
    mine = jnp.concatenate(add_all(parts, moved), axis=0)
    other = lax.ppermute(mine, "row", CORE_SWAP)
    for_mine, for_other = columns_of(inverse, core), columns_of(inverse, 1 - core)
    r_mine = jnp.dot(for_mine, mine, precision=HIGH)
    ordered = jnp.concatenate([for_other, for_mine], axis=1)
    basis = jnp.dot(panels, ordered.T * root_rows, precision=HIGH)
    other, r_mine, basis = tie(other, r_mine, basis)
    r_rows = r_mine + jnp.dot(for_other, other, precision=HIGH)
    trailing = matrix - jnp.dot(basis, r_rows * (1.0 / root_rows), precision=HIGH)
    return (r_rows, basis, trailing)


def solution(mesh):
    placed = (P("row", "col"),)
    return jax.shard_map(
        on_device,
        mesh=mesh,
        in_specs=placed,
        out_specs=(P(None, "col"), P("row", None), P("row", "col")),
        check_vma=False,
    )
```

```python
import functools
import math

import jax
import jax.numpy as jnp
from jax import lax
from jax.experimental import pallas as pl
from jax.experimental.pallas import tpu as pltpu
from jax.sharding import PartitionSpec as P

B = 256
PANELS = 2
SIDE = 4
BLOCK = 128
SUB = 8
STRIDE = 2


HIGHEST = lax.Precision.HIGHEST
HIGH = lax.Precision.HIGH
CORE_SWAP = [(i, i ^ 1) for i in range(2 * SIDE)]
PAIRS_A = [(2 * x + c, 2 * (x ^ 1) + c) for x in range(SIDE) for c in range(2)]
PAIRS_B = [(2 * x + c, 2 * (3 - x) + c) for x in range(SIDE) for c in range(2)]


def ring(axis, step):
    if axis == "y":
        return [(z * SIDE + y, z * SIDE + (y + step) % SIDE) for z in range(SIDE) for y in range(SIDE)]
    return [(z * SIDE + y, (z + step) % SIDE * SIDE + y) for z in range(SIDE) for y in range(SIDE)]


def half_of(x, upper):
    half = x.shape[0] // 2
    return lax.dynamic_slice_in_dim(x, upper * half, half, 0)


def tie(*values):
    return lax.optimization_barrier(values)


def swap_start(parts, swap_1, swap_2):
    return lax.ppermute(parts[0], "row", swap_1), lax.ppermute(parts[1], "row", swap_2)


def add_all(mine, theirs):
    return [a + b for a, b in zip(mine, theirs)]


def split(x):
    half = x.shape[0] // 2
    return x[:half], x[half:]


def scatter(matrix):
    col = lax.axis_index("col")
    first_core = lax.axis_index("row") % 2 == 0
    count = SIDE * SIDE
    rows = matrix.shape[0] // count
    before = (col + count - 1) % count
    step_1 = jnp.where(first_core, before, col)
    step_2 = jnp.where(first_core, col, before)
    mine = lax.dynamic_slice(matrix, (col * rows, 0), (rows, B))
    slot_1 = jnp.where(step_1 == 0, mine, 0.0)
    slot_2 = jnp.where(step_2 == 0, mine, 0.0)
    for i in range(1, count):
        piece = lax.dynamic_slice(matrix, ((i + col) % count * rows, 0), (rows, B))
        got = lax.ppermute(piece, "col", [(0, i), (1, (i + 1) % count)])
        slot_1 = jnp.where(step_1 == i, got, slot_1)
        slot_2 = jnp.where(step_2 == i, got, slot_2)
    return jnp.concatenate([slot_1, slot_2], axis=1)


def ring_gather(x, axis):
    half = x.shape[0] // 2
    before = lax.ppermute(x, "col", ring(axis, 1))
    after = lax.ppermute(x, "col", ring(axis, -1))
    far_1 = lax.ppermute(before[:half], "col", ring(axis, 1))
    far_2 = lax.ppermute(after[half:], "col", ring(axis, -1))
    return [x, after, jnp.concatenate([far_1, far_2], axis=0), before]


def place_gather(x, axis, spot):
    pieces = ring_gather(x, axis)
    out = jnp.zeros((SIDE,) + x.shape, x.dtype)
    for step, piece in enumerate(pieces):
        out = lax.dynamic_update_index_in_dim(out, piece, (spot + step) % SIDE, 0)
    return out


def gather_panels(piece):
    col = lax.axis_index("col")
    y = col % SIDE
    z = col // SIDE
    rows, width = piece.shape
    half = rows // 2
    part_a = place_gather(piece[:half], "y", y)
    part_b = place_gather(piece[half:], "z", z)
    part_a = place_gather(part_a.reshape(SIDE * half, width), "z", z)
    part_b = place_gather(part_b.reshape(SIDE * half, width), "y", y)
    part_a = part_a.reshape(SIDE, SIDE, 1, half, width)
    part_b = part_b.reshape(SIDE, SIDE, 1, half, width).transpose(1, 0, 2, 3, 4)
    return jnp.concatenate([part_a, part_b], axis=2).reshape(SIDE * SIDE * rows, width)


def inverse_factor_kernel(first_block, last, core_ref, state_ref, out_ref, block):
    size = state_ref.shape[0]
    out_ref[...] = state_ref[...]
    lane = lax.broadcasted_iota(jnp.int32, (SUB, BLOCK), 1)
    sub = lax.broadcasted_iota(jnp.int32, (SUB, BLOCK), 0)
    tiles_n = BLOCK // SUB
    low = first_block * BLOCK
    span = size - low

    def panel_steps(begin, end):
        tiles = {t: block[t * SUB:(t + 1) * SUB, :] for t in range(begin, tiles_n)}
        for a in range(begin, end):
            first = a * SUB
            in_panel = (lane >= first) & (lane < first + SUB)
            panel = jnp.where(in_panel, 0.0, tiles[a])
            cols = [jnp.broadcast_to(tiles[a][:, first + s:first + s + 1], (SUB, BLOCK)) for s in range(SUB)]
            pivots = jnp.zeros((SUB, BLOCK), jnp.float32)
            scaled, ratios = [], {}
            for s in range(SUB):
                pivot = jnp.broadcast_to(cols[s][s:s + 1, :], (SUB, BLOCK))
                pivots = jnp.where(sub == s, pivot, pivots)
                inverse = pl.reciprocal(pivot, approx=False)
                row = jnp.broadcast_to(panel[s:s + 1, :], (SUB, BLOCK))
                scaled.append(jnp.where(lane == first + s, 1.0, row) * inverse)
                factor = jnp.where(sub > s, cols[s], 0.0)
                for u in range(s + 1, SUB):
                    ratios[s, u] = jnp.broadcast_to(cols[u][s:s + 1, :], (SUB, BLOCK)) * inverse
                    cols[u] = cols[u] - factor * ratios[s, u]
                panel = panel - factor * scaled[s]
            root = lax.rsqrt(pivots)
            root = root * (1.5 - 0.5 * pivots * root * root)
            lower = jnp.where(lane < sub + first, panel, 0.0)
            block[first:first + SUB, :] = jnp.where(lane == sub + first, 1.0, lower) * root
            for t in range(a + 1, tiles_n):
                cols = [jnp.broadcast_to(tiles[t][:, first + s:first + s + 1], (SUB, BLOCK)) for s in range(SUB)]
                tile = jnp.where(in_panel, 0.0, tiles[t])
                for s in range(SUB):
                    for u in range(s + 1, SUB):
                        cols[u] = cols[u] - cols[s] * ratios[s, u]
                    tile = tile - cols[s] * scaled[s]
                tiles[t] = tile
        for t in range(end, tiles_n):
            block[t * SUB:(t + 1) * SUB, :] = tiles[t]

    def block_step(k, carry):
        start = pl.multiple_of(k * BLOCK, BLOCK)
        block[...] = out_ref[pl.ds(start, BLOCK), pl.ds(start, BLOCK)]
        for begin in range(0, tiles_n, STRIDE):
            pl.when(k >= 0)(functools.partial(panel_steps, begin, begin + STRIDE))
        strip = jnp.dot(block[...], out_ref[pl.ds(start, BLOCK), :], precision=HIGHEST, preferred_element_type=jnp.float32)
        out_ref[pl.ds(start, BLOCK), :] = strip
        out_ref[pl.ds(start, BLOCK), pl.ds(start, BLOCK)] = block[...]
        full = out_ref[pl.ds(start, BLOCK), :]
        row_id = low + lax.broadcasted_iota(jnp.int32, (span, size), 0)
        col_id = lax.broadcasted_iota(jnp.int32, (span, size), 1)
        change = lax.dot_general(
            strip[:, low:], full, (((0,), (0,)), ((), ())), precision=HIGHEST, preferred_element_type=jnp.float32)
        in_block = (col_id >= start) & (col_id < start + BLOCK)
        now = out_ref[low:, :]
        out_ref[low:, :] = jnp.where(row_id >= start + BLOCK, jnp.where(in_block, 0.0, now) - change, now)
        return carry

    lax.fori_loop(first_block, last, block_step, 0)
    if last * BLOCK == size:
        row_id = lax.broadcasted_iota(jnp.int32, (size, size), 0)
        col_id = lax.broadcasted_iota(jnp.int32, (size, size), 1)
        lower = jnp.where(row_id >= col_id, out_ref[...], 0.0)
        half = size // 2
        swapped = jnp.concatenate([lower[:, half:], lower[:, :half]], axis=1)
        out_ref[...] = jnp.where(core_ref[0] == 0, swapped, lower)


def factor_part(core, state, first_block, last):
    size = state.shape[0]
    return pl.pallas_call(
        functools.partial(inverse_factor_kernel, first_block, last),
        out_shape=jax.ShapeDtypeStruct((size, size), jnp.float32),
        in_specs=[pl.BlockSpec(memory_space=pltpu.SMEM), pl.BlockSpec(memory_space=pltpu.VMEM)],
        out_specs=pl.BlockSpec(memory_space=pltpu.VMEM),
        scratch_shapes=[pltpu.VMEM((BLOCK, BLOCK), jnp.float32)],
        cost_estimate=pl.CostEstimate(flops=6 * 10**9, transcendentals=0, bytes_accessed=2 * 10**6),
        name=f"inverse_factor_{first_block}",
    )(core.reshape(1), state)


def on_device(matrix):
    root_rows = math.sqrt(matrix.shape[0] * lax.axis_size("row"))
    panels = gather_panels(scatter(matrix))
    core = lax.axis_index("row") % 2
    first_core = core == 0
    gram = jnp.dot(panels.T, panels, precision=HIGHEST)
    cross = jnp.where(first_core, gram[B:, :B], gram[:B, B:])
    kept = jnp.concatenate([gram[B:, B:], half_of(cross, core)], axis=0)
    sent = jnp.concatenate([gram[:B, :B], half_of(cross, 1 - core)], axis=0)
    gram = split(kept + lax.ppermute(sent, "row", CORE_SWAP))
    moved = swap_start(gram, PAIRS_A, PAIRS_B)
    coupling = jnp.dot(panels.T, matrix, precision=HIGH)
    moved, coupling = tie(moved, coupling)
    gram = add_all(gram, moved)
    other, mine = split(coupling)
    moved = swap_start(gram, PAIRS_B, PAIRS_A)
    mine = mine + lax.ppermute(other, "row", CORE_SWAP)
    moved, mine = tie(moved, mine)
    gram = jnp.concatenate(add_all(gram, moved), axis=0)
    mine, gram = tie(mine, gram)
    theirs = lax.ppermute(gram, "row", CORE_SWAP)
    left, right = jnp.where(first_core, gram, theirs), jnp.where(first_core, theirs, gram)
    cross = jnp.concatenate([left[B:], right[B:]], axis=0)
    full = jnp.concatenate([
        jnp.concatenate([left[:B], cross], axis=1),
        jnp.concatenate([cross, right[:B]], axis=1)], axis=0)
    middle = full.shape[0] // BLOCK // 2
    parts = split(mine)
    moved = swap_start(parts, PAIRS_A, PAIRS_B)
    state = factor_part(core, full, 0, middle)
    moved, state = tie(moved, state)
    parts = add_all(parts, moved)
    moved = swap_start(parts, PAIRS_B, PAIRS_A)
    inverse = factor_part(core, state, middle, 2 * middle)
    moved, inverse = tie(moved, inverse)
    mine = jnp.concatenate(add_all(parts, moved), axis=0)
    other = lax.ppermute(mine, "row", CORE_SWAP)
    for_other, for_mine = inverse[:, :B], inverse[:, B:]
    r_mine = jnp.dot(for_mine, mine, precision=HIGH)
    basis = jnp.dot(panels, inverse.T * root_rows, precision=HIGH)
    other, r_mine, basis = tie(other, r_mine, basis)
    r_rows = r_mine + jnp.dot(for_other, other, precision=HIGH)
    trailing = matrix - jnp.dot(basis, r_rows * (1.0 / root_rows), precision=HIGH)
    return (r_rows, basis, trailing)


def solution(mesh):
    placed = (P("row", "col"),)
    return jax.shard_map(
        on_device,
        mesh=mesh,
        in_specs=placed,
        out_specs=(P(None, "col"), P("row", None), P("row", "col")),
        check_vma=False,
    )
```
